32 devices in a mesh: plane: 2 (over x), coil: 16 (over z, y, core).
Axes of the slice: x: 2, y: 2, z: 4, core: 2. Of those that a mesh axis runs over, the one named last changes fastest.
Arguments:
- image: float32 [512, 8, 512], P(('plane', 'coil')), parts along dimension 0, may hold values from -6 to 6
- sens: float32 [512, 32, 512], P(('plane', 'coil')), parts along dimension 0, may hold values from -0.75 to 0.75
- kspace: float32 [512, 256, 512], P('plane', 'coil'), parts along dimension 0, may hold values from -6 to 6
- mask: int32 [8, 256], replicated, may hold values 0 or 1
Outputs:
- recon: float32 [512, 8, 512], P(('plane', 'coil')), parts along dimension 0
The draws below stay inside these ranges and needn't reach their ends.
There are 2 independent parts, one for each index of `plane`. The reference program is written for one: setup_inputs(seed, part) draws one part's arguments, and reference() takes and returns one part's arrays. A program takes and returns all parts, laid end to end along the dimension named above; an argument that names none is the same for every part. Nothing has to cross between parts.
Inputs may be any that keep to these rules, and one draw needn't show every extreme that they name: mask[f, ky] is 1 where phase-encode line ky is sampled in frame f, else 0.
All inputs are finite; a program needn't handle non-finite values.
Results may differ from the reference program's by a relative error of at most 0.0001.
Values sent between devices are 32-bit elements; how exact they have to be, the bound alone decides.
A program may use at most 128 MiB of HBM per device.

```python
import jax
import jax.numpy as jnp
from jax import lax

NY = 256
NZ = 256
COILS = 32
FRAMES = 8
OUTER = 2
INNER = 2


def plant(array, rng, least, top_value):
    spot = [jax.random.randint(jax.random.fold_in(rng, axis), (), 0, length) for axis, length in enumerate(array.shape)]
    longest = array.shape.index(max(array.shape))
    neighbour = spot[:longest] + [(spot[longest] + 1) % array.shape[longest]] + spot[longest + 1:]
    return array.at[tuple(spot)].set(least).at[tuple(neighbour)].set(top_value)


def steps_of(rng, extent, shards, low, top_value):
    level, own = 1.0, jax.random.fold_in(rng, 6)
    for axis_at, parts in shards:
        steps = jnp.exp(jax.random.uniform(jax.random.fold_in(own, axis_at), (parts,), jnp.float32, low / len(shards), top_value / len(shards)))
        level = level * jnp.repeat(steps, extent[axis_at] // parts).reshape([-1 if axis == axis_at else 1 for axis in range(len(extent))])
    return level


def centred(rng, dims, width, limit, cuts=(), held_as=jnp.bfloat16):
    level = steps_of(rng, dims, cuts, -0.22, 0.18) if cuts else 1.0
    values = jax.random.normal(rng, dims, jnp.float32) * width * level
    return jnp.minimum(jnp.maximum(values, -limit), limit).astype(held_as)


def setup_inputs(seed: int = 0, part: int = 0) -> dict:
    splits = jax.random.split(jax.random.key(seed), 5)
    part_splits = jax.random.split(jax.random.fold_in(splits[4], part), 5)
    return {
        "image": centred(part_splits[0], (NY, FRAMES, 2 * NZ), 1.0, 6.0, ((0, 16),), jnp.float32),
        "sens": centred(part_splits[1], (NY, COILS, 2 * NZ), 0.125, 0.75, ((0, 16),), jnp.float32),
        "kspace": centred(part_splits[2], (NY, COILS * FRAMES, 2 * NZ), 1.0, 6.0, ((1, 16),), jnp.float32),
        "mask": plant((jax.random.randint(splits[3], (FRAMES, NY), 0, 3) < 1).astype(jnp.int32), jax.random.fold_in(splits[3], 1), 0, 1),
    }


step_size = 0.5
tv_weight = 0.1
dual_step = 1.25


def unpack_complex(packed):
    half = packed.shape[-1] // 2
    return lax.complex(packed[..., :half], packed[..., half:])


def pack_complex(values):
    return jnp.concatenate([jnp.real(values), jnp.imag(values)], -1)


def forward_diff(field):
    diff_rows = jnp.concatenate([field[1:] - field[:-1], jnp.zeros_like(field[:1])], 0)
    diff_time = jnp.concatenate([field[:, 1:] - field[:, :-1], jnp.zeros_like(field[:, :1])], 1)
    return diff_time, diff_rows


def adjoint_diff(dual_time, dual_rows):
    keep_time = (lax.iota(jnp.int32, dual_time.shape[1]) < dual_time.shape[1] - 1)[None, :, None]
    keep_rows = (lax.iota(jnp.int32, dual_rows.shape[0]) < dual_rows.shape[0] - 1)[:, None, None]
    from_time = jnp.concatenate([jnp.zeros_like(dual_time[:, :1]), dual_time[:, :-1]], 1) - jnp.where(keep_time, dual_time, 0.0)
    from_rows = jnp.concatenate([jnp.zeros_like(dual_rows[:1]), dual_rows[:-1]], 0) - jnp.where(keep_rows, dual_rows, 0.0)
    return from_time + from_rows


def reference(image, sens, kspace, mask):
    maps = jnp.transpose(unpack_complex(sens), (1, 0, 2))
    data = jnp.transpose(unpack_complex(kspace).reshape(NY, COILS, FRAMES, NZ), (1, 2, 0, 3))
    sampled = mask.astype(jnp.float32)[:, :, None]
    field = image
    for sweep in range(OUTER):
        frames_now = jnp.transpose(unpack_complex(field), (1, 0, 2))

        def add_coil(total, coil_input):
            coil_map, coil_data = coil_input
            spectrum = jnp.fft.fft2(coil_map[None] * frames_now, axes=(1, 2), norm="ortho")
            residual = sampled * (spectrum - coil_data)
            term = jnp.conj(coil_map)[None] * jnp.fft.ifft2(residual, axes=(1, 2), norm="ortho")
            return total + term, None

        total, unused = lax.scan(add_coil, jnp.zeros_like(frames_now), (maps, data))
        gradient = pack_complex(jnp.transpose(total, (1, 0, 2)))
        target = field - step_size * gradient
        dual_time = jnp.zeros_like(target)
        dual_rows = jnp.zeros_like(target)
        for repeat in range(INNER):
            primal = target - tv_weight * adjoint_diff(dual_time, dual_rows)
            diff_time, diff_rows = forward_diff(primal)
            dual_time = jnp.clip(dual_time + dual_step * diff_time, -1.0, 1.0)
            dual_rows = jnp.clip(dual_rows + dual_step * diff_rows, -1.0, 1.0)
        field = target - tv_weight * adjoint_diff(dual_time, dual_rows)
    return field
```

```python
import jax
import jax.numpy as jnp
from jax import lax
from jax.sharding import PartitionSpec as P

OUTER = 2
INNER = 2

step_size = 0.5
tv_weight = 0.1
dual_step = 1.25
high = lax.Precision.HIGH


def contract(spec, *operands):
    return jnp.einsum(spec, *operands, precision=high, preferred_element_type=jnp.float32)


def dft_tables(length):
    index = lax.iota(jnp.int32, length)
    product = index[:, None] * index[None, :] % length
    angle = 2.0 * jnp.pi / length * product.astype(jnp.float32)
    scale = 1.0 / jnp.sqrt(jnp.float32(length))
    return (jnp.cos(angle) * scale, -jnp.sin(angle) * scale)


def column_matrix(cos_part, sin_part):
    upper = jnp.concatenate([cos_part, sin_part], 1)
    lower = jnp.concatenate([-sin_part, cos_part], 1)
    return jnp.concatenate([upper, lower], 0)


def projections(mask, row_cos, row_sin):
    weights = mask.astype(jnp.float32)
    wide = jnp.concatenate([row_cos, row_sin], 1)
    cos_rows = weights[:, :, None] * row_cos[None]
    sin_rows = weights[:, :, None] * row_sin[None]
    from_cos = contract("fka,ky->fay", cos_rows, wide)
    from_sin = contract("fka,ky->fay", sin_rows, wide)
    length = row_cos.shape[0]
    real = from_cos[..., :length] + from_sin[..., length:]
    imag = from_cos[..., length:] - from_sin[..., :length]
    return (real, imag)


def to_columns(field, devices):
    rows, count, packed = field.shape
    width = packed // 2 // devices
    parts = field.reshape(rows, count, 2, devices, width)
    return jnp.transpose(parts, (3, 0, 2, 1, 4)).reshape(devices, rows, 2 * count * width)


def divergence(dual_time, dual_rows):
    time_axis, row_axis = 1, 3
    zero_time = jnp.zeros_like(dual_time[:, :1])
    zero_rows = jnp.zeros_like(dual_rows[..., :1])
    head_time = dual_time[:, :-1]
    head_rows = dual_rows[..., :-1]
    from_time = jnp.concatenate([zero_time, head_time], time_axis) - jnp.concatenate(
        [head_time, zero_time], time_axis
    )
    from_rows = jnp.concatenate([zero_rows, head_rows], row_axis) - jnp.concatenate(
        [head_rows, zero_rows], row_axis
    )
    return from_time + from_rows


def forward_diff(field):
    diff_time = jnp.concatenate(
        [field[:, 1:] - field[:, :-1], jnp.zeros_like(field[:, :1])], 1
    )
    diff_rows = jnp.concatenate(
        [field[..., 1:] - field[..., :-1], jnp.zeros_like(field[..., :1])], 3
    )
    return (diff_time, diff_rows)


def denoise(target):
    dual_time = jnp.zeros_like(target)
    dual_rows = jnp.zeros_like(target)
    for repeat in range(INNER):
        primal = target
        if repeat:
            primal = target - tv_weight * divergence(dual_time, dual_rows)
        diff_time, diff_rows = forward_diff(primal)
        dual_time = jnp.clip(dual_time + dual_step * diff_time, -1.0, 1.0)
        dual_rows = jnp.clip(dual_rows + dual_step * diff_rows, -1.0, 1.0)
    return target - tv_weight * divergence(dual_time, dual_rows)


def iterate(field, data_term, maps, real, imag):
    maps_re, maps_im = (maps[0][None], maps[1][None])
    for sweep in range(OUTER):
        now_re, now_im = (field[0][:, None], field[1][:, None])
        seen_re = maps_re * now_re - maps_im * now_im
        seen_im = maps_re * now_im + maps_im * now_re
        kept_re = contract("fczy,fky->fczk", seen_re, real) - contract(
            "fczy,fky->fczk", seen_im, imag
        )
        kept_im = contract("fczy,fky->fczk", seen_re, imag) + contract(
            "fczy,fky->fczk", seen_im, real
        )
        grad_re = jnp.sum(maps_re * kept_re + maps_im * kept_im, 1)
        grad_im = jnp.sum(maps_re * kept_im - maps_im * kept_re, 1)
        gradient = jnp.stack([grad_re, grad_im]) - data_term
        field = denoise(field - step_size * gradient)
    return field


def data_images(kspace, mask_pairs, row_cos, row_sin, col_cos, col_sin):
    masked = jnp.transpose(mask_pairs)[:, :, None] * kspace
    mid = contract("kpz,zw->kpw", masked, column_matrix(col_cos, -col_sin))
    half = kspace.shape[-1] // 2
    from_cos = contract("ky,kpz->ypz", row_cos, mid)
    from_sin = contract("ky,kpz->ypz", row_sin, mid)
    real = from_cos[..., :half] + from_sin[..., half:]
    imag = from_cos[..., half:] - from_sin[..., :half]
    return (real, imag)


def per_device(image, sens, kspace, mask):
    devices = lax.axis_size("coil")
    device = lax.axis_index("coil")
    rows_dev, frames, packed = image.shape
    coils = sens.shape[1]
    length, pairs, unused = kspace.shape
    half = packed // 2
    width = half // devices
    copies = max(1, frames // pairs)
    own_coils = max(1, pairs // frames)
    own_frames = min(frames, pairs)
    row_cos, row_sin = dft_tables(length)
    col_cos, col_sin = dft_tables(half)

    spread = sens if copies == 1 else jnp.repeat(sens, copies, axis=1)
    own_maps = lax.all_to_all(spread, "coil", split_axis=1, concat_axis=0, tiled=True)
    outgoing = jnp.concatenate([to_columns(sens, devices), to_columns(image, devices)], 2)
    incoming = lax.all_to_all(outgoing, "coil", split_axis=0, concat_axis=0, tiled=True)
    columns = jnp.transpose(incoming.reshape(length, -1))
    cut = 2 * coils * width
    maps = columns[:cut].reshape(2, coils, width, length)
    field = columns[cut:].reshape(2, frames, width, length)

    first_frame = device * pairs % frames
    mask_float = mask.astype(jnp.float32)
    local_mask = lax.dynamic_slice_in_dim(mask_float, first_frame, own_frames, 0)
    mask_pairs = jnp.tile(local_mask, (own_coils, 1))
    base_re, base_im = data_images(kspace, mask_pairs, row_cos, row_sin, col_cos, col_sin)
    base_re = base_re.reshape(length, own_coils, own_frames, half)
    base_im = base_im.reshape(length, own_coils, own_frames, half)
    own_re, own_im = (own_maps[:, :, None, :half], own_maps[:, :, None, half:])
    term_re = jnp.sum(own_re * base_re + own_im * base_im, 1)
    term_im = jnp.sum(own_re * base_im - own_im * base_re, 1)
    term = jnp.transpose(jnp.stack([term_re, term_im]), (3, 0, 2, 1))
    if own_frames < frames:
        wide = jnp.zeros((half, 2, frames, length), jnp.float32)
        term = lax.dynamic_update_slice_in_dim(wide, term, first_frame, 2)
    term = term.reshape(devices, width, 2, frames, length)
    data_term = lax.psum_scatter(term, "coil", scatter_dimension=0, tiled=True)
    data_term = jnp.transpose(data_term[0], (1, 2, 0, 3))

    real, imag = projections(mask, row_cos, row_sin)
    field = iterate(field, data_term, maps, real, imag)

    leaving = jnp.transpose(field.reshape(2 * frames * width, length))
    leaving = leaving.reshape(devices, rows_dev, 2 * frames * width)
    arrived = lax.all_to_all(leaving, "coil", split_axis=0, concat_axis=0, tiled=True)
    arrived = arrived.reshape(devices, rows_dev, 2, frames, width)
    return jnp.transpose(arrived, (1, 3, 2, 0, 4)).reshape(rows_dev, frames, packed)


def solution(mesh):
    return jax.shard_map(
        per_device,
        mesh=mesh,
        in_specs=(
            P(("plane", "coil"), None, None),
            P(("plane", "coil"), None, None),
            P("plane", "coil", None),
            P(),
        ),
        out_specs=P(("plane", "coil"), None, None),
        check_vma=False,
    )
```

```python
import jax
import jax.numpy as jnp
from jax import lax
from jax.experimental import pallas as pl
from jax.experimental.pallas import tpu as pltpu
from jax.sharding import PartitionSpec as P

OUTER = 2
INNER = 2

step_size = 0.5
tv_weight = 0.1
dual_step = 1.25
high = lax.Precision.HIGH


def contract(spec, *operands):
    return jnp.einsum(spec, *operands, precision=high, preferred_element_type=jnp.float32)


def dft_tables(length):
    index = lax.iota(jnp.int32, length)
    product = index[:, None] * index[None, :] % length
    angle = 2.0 * jnp.pi / length * product.astype(jnp.float32)
    scale = 1.0 / jnp.sqrt(jnp.float32(length))
    return (jnp.cos(angle) * scale, -jnp.sin(angle) * scale)


def column_matrix(cos_part, sin_part):
    upper = jnp.concatenate([cos_part, sin_part], 1)
    lower = jnp.concatenate([-sin_part, cos_part], 1)
    return jnp.concatenate([upper, lower], 0)


def projections(mask, row_cos, row_sin):
    weights = mask.astype(jnp.float32)
    wide = jnp.concatenate([row_cos, row_sin], 1)
    cos_rows = weights[:, :, None] * row_cos[None]
    sin_rows = weights[:, :, None] * row_sin[None]
    from_cos = contract("fka,ky->fay", cos_rows, wide)
    from_sin = contract("fka,ky->fay", sin_rows, wide)
    length = row_cos.shape[0]
    real = from_cos[..., :length] + from_sin[..., length:]
    imag = from_cos[..., length:] - from_sin[..., :length]
    return (real, imag)


def to_columns(field, devices):
    rows, count, packed = field.shape
    width = packed // 2 // devices
    parts = field.reshape(rows, count, 2, devices, width)
    return jnp.transpose(parts, (3, 0, 2, 1, 4)).reshape(devices, rows, 2 * count * width)


def divergence(dual_time, dual_rows):
    time_axis, row_axis = 1, 3
    zero_time = jnp.zeros_like(dual_time[:, :1])
    zero_rows = jnp.zeros_like(dual_rows[..., :1])
    head_time = dual_time[:, :-1]
    head_rows = dual_rows[..., :-1]
    from_time = jnp.concatenate([zero_time, head_time], time_axis) - jnp.concatenate(
        [head_time, zero_time], time_axis
    )
    from_rows = jnp.concatenate([zero_rows, head_rows], row_axis) - jnp.concatenate(
        [head_rows, zero_rows], row_axis
    )
    return from_time + from_rows


def forward_diff(field):
    diff_time = jnp.concatenate(
        [field[:, 1:] - field[:, :-1], jnp.zeros_like(field[:, :1])], 1
    )
    diff_rows = jnp.concatenate(
        [field[..., 1:] - field[..., :-1], jnp.zeros_like(field[..., :1])], 3
    )
    return (diff_time, diff_rows)


def denoise(target):
    dual_time = jnp.zeros_like(target)
    dual_rows = jnp.zeros_like(target)
    for repeat in range(INNER):
        primal = target
        if repeat:
            primal = target - tv_weight * divergence(dual_time, dual_rows)
        diff_time, diff_rows = forward_diff(primal)
        dual_time = jnp.clip(dual_time + dual_step * diff_time, -1.0, 1.0)
        dual_rows = jnp.clip(dual_rows + dual_step * diff_rows, -1.0, 1.0)
    return target - tv_weight * divergence(dual_time, dual_rows)


def iterate(field, data_term, maps, real, imag):
    maps_re, maps_im = (maps[0][None], maps[1][None])
    for sweep in range(OUTER):
        now_re, now_im = (field[0][:, None], field[1][:, None])
        seen_re = maps_re * now_re - maps_im * now_im
        seen_im = maps_re * now_im + maps_im * now_re
        kept_re = contract("fczy,fky->fczk", seen_re, real) - contract(
            "fczy,fky->fczk", seen_im, imag
        )
        kept_im = contract("fczy,fky->fczk", seen_re, imag) + contract(
            "fczy,fky->fczk", seen_im, real
        )
        grad_re = jnp.sum(maps_re * kept_re + maps_im * kept_im, 1)
        grad_im = jnp.sum(maps_re * kept_im - maps_im * kept_re, 1)
        gradient = jnp.stack([grad_re, grad_im]) - data_term
        field = denoise(field - step_size * gradient)
    return field


def data_images(kspace, mask_pairs, row_cos, row_sin, col_cos, col_sin):
    masked = jnp.transpose(mask_pairs)[:, :, None] * kspace
    mid = contract("kpz,zw->kpw", masked, column_matrix(col_cos, -col_sin))
    half = kspace.shape[-1] // 2
    from_cos = contract("ky,kpz->ypz", row_cos, mid)
    from_sin = contract("ky,kpz->ypz", row_sin, mid)
    real = from_cos[..., :half] + from_sin[..., half:]
    imag = from_cos[..., half:] - from_sin[..., :half]
    return (real, imag)


LANES = 128
SUBLANES = 8


def swap_blocks(values, width):
    count = len(values)
    block = lax.broadcasted_iota(jnp.int32, values[0].shape, 1) // width
    step = count // 2
    while step:
        lower = block // step % 2 == 0
        shift = step * width
        values = list(values)
        for at in range(count):
            if at // step % 2 == 0:
                near, far = (values[at], values[at + step])
                values[at] = jnp.where(lower, near, pltpu.roll(far, shift, 1))
                values[at + step] = jnp.where(lower, pltpu.roll(near, LANES - shift, 1), far)
        step //= 2
    return values


def blocked(devices, width, rows, counts):
    group = LANES // width
    fits = LANES % width == 0 and width % SUBLANES == 0 and rows % SUBLANES == 0
    return fits and devices % group == 0 and all(count % group == 0 for count in counts)


def pack_kernel(devices, width, sens_ref, image_ref, out_ref):
    group = LANES // width
    half = devices * width
    start = 0
    for source in (sens_ref, image_ref):
        count = source.shape[1]
        for part in range(2):
            for tile in range(half // LANES):
                lane = part * half + tile * LANES
                for first in range(0, count, group):
                    taken = [source[:, first + at, lane : lane + LANES] for at in range(group)]
                    target = start + (part * count + first) * width
                    for at, value in enumerate(swap_blocks(taken, width)):
                        out_ref[tile * group + at, :, target : target + LANES] = value
        start += 2 * count * width


def pack_columns(sens, image, devices):
    rows, coils, packed = sens.shape
    frames = image.shape[1]
    width = packed // 2 // devices
    if not blocked(devices, width, rows, (coils, frames)):
        return jnp.concatenate([to_columns(sens, devices), to_columns(image, devices)], 2)
    return pl.pallas_call(
        lambda *refs: pack_kernel(devices, width, *refs),
        out_shape=jax.ShapeDtypeStruct((devices, rows, 2 * (coils + frames) * width), jnp.float32),
        in_specs=[pl.BlockSpec(memory_space=pltpu.VMEM)] * 2,
        out_specs=pl.BlockSpec(memory_space=pltpu.VMEM),
        name="pack_columns",
    )(sens, image)


def greet(peers):
    barrier = pltpu.get_barrier_semaphore()
    for peer in peers:
        pl.semaphore_signal(barrier, 1, device_id={"coil": peer}, device_id_type=MESH)
    pl.semaphore_wait(barrier, len(peers))


MESH = pl.DeviceIdType.MESH


def reduce_kernel(
    devices, term_ref, out_ref, got_a, sum_a, got_b, sum_b, got_c, send_sem, recv_sem
):
    frames = term_ref.shape[0]
    width = out_ref.shape[2]
    ranks = devices // 4
    me = lax.axis_index("coil")
    core = me % 2
    side = me // 2 % 2
    rank = me // 4
    core_peer = me + 1 - 2 * core
    side_peer = me + 2 - 4 * side
    rank_peers = [(me + 4 * hop) % devices for hop in range(1, ranks)]
    greet([core_peer, side_peer] + rank_peers)

    def copy_to(source, target, frame, slot, peer):
        return pltpu.make_async_remote_copy(
            src_ref=source,
            dst_ref=target,
            send_sem=send_sem.at[frame, slot],
            recv_sem=recv_sem.at[frame, slot],
            device_id={"coil": peer},
            device_id_type=MESH,
        )

    def core_copy(frame):
        return copy_to(term_ref.at[frame, :, :, 1 - core], got_a.at[frame], frame, 0, core_peer)

    def side_copy(frame):
        return copy_to(sum_a.at[frame, :, 1 - side], got_b.at[frame], frame, 1, side_peer)

    def rank_copy(frame, hop):
        return copy_to(
            sum_b.at[frame, (rank + hop) % ranks],
            got_c.at[frame, hop - 1],
            frame,
            1 + hop,
            rank_peers[hop - 1],
        )

    for frame in range(frames):
        core_copy(frame).start()
    for turn in range(frames + 2):
        if turn < frames:
            frame = turn
            core_copy(frame).wait()
            sum_a[frame] = term_ref[frame, :, :, core] + got_a[frame]
            side_copy(frame).start()
        if 0 <= turn - 1 < frames:
            frame = turn - 1
            side_copy(frame).wait()
            sum_b[frame] = sum_a[frame, :, side] + got_b[frame]
            for hop in range(1, ranks):
                rank_copy(frame, hop).start()
        if turn - 2 >= 0:
            frame = turn - 2
            total = sum_b[frame, rank]
            for hop in range(1, ranks):
                rank_copy(frame, hop).wait()
                total = total + got_c[frame, hop - 1]
            out_ref[0, frame] = total[:width]
            out_ref[1, frame] = total[width:]


def reduce_columns(term, devices, width):
    frames, unused, unused, length = term.shape
    ranks = devices // 4
    flat = term.reshape(frames, ranks, 2, 2, 2 * width, length)
    return pl.pallas_call(
        lambda *refs: reduce_kernel(devices, *refs),
        out_shape=jax.ShapeDtypeStruct((2, frames, width, length), jnp.float32),
        in_specs=[pl.BlockSpec(memory_space=pltpu.VMEM)],
        out_specs=pl.BlockSpec(memory_space=pltpu.VMEM),
        scratch_shapes=[
            pltpu.VMEM((frames, ranks, 2, 2 * width, length), jnp.float32),
            pltpu.VMEM((frames, ranks, 2, 2 * width, length), jnp.float32),
            pltpu.VMEM((frames, ranks, 2 * width, length), jnp.float32),
            pltpu.VMEM((frames, ranks, 2 * width, length), jnp.float32),
            pltpu.VMEM((frames, ranks - 1, 2 * width, length), jnp.float32),
            pltpu.SemaphoreType.DMA((frames, ranks + 1)),
            pltpu.SemaphoreType.DMA((frames, ranks + 1)),
        ],
        compiler_params=pltpu.CompilerParams(collective_id=0, has_side_effects=True),
        name="reduce_columns",
    )(flat)


def return_kernel(devices, width, field_ref, out_ref, ready, landed, send_sem, recv_sem):
    rows, frames, unused = out_ref.shape
    group = LANES // width
    half = devices * width
    me = lax.axis_index("coil")
    peers = [(me + hop) % devices for hop in range(1, devices)]
    turned = jnp.transpose(field_ref[...])
    ready[...] = turned.reshape(devices, rows, turned.shape[1])
    greet(peers)
    copies = []
    for hop in range(1, devices):
        copies.append(
            pltpu.make_async_remote_copy(
                src_ref=ready.at[peers[hop - 1]],
                dst_ref=landed.at[me],
                send_sem=send_sem.at[hop - 1],
                recv_sem=recv_sem.at[hop - 1],
                device_id={"coil": peers[hop - 1]},
                device_id_type=MESH,
            )
        )
        copies[-1].start()
    landed[me] = ready[me]
    for copy in copies:
        copy.wait()
    for part in range(2):
        for first in range(0, frames, group):
            lane = (part * frames + first) * width
            for tile in range(devices // group):
                taken = [landed[tile * group + at, :, lane : lane + LANES] for at in range(group)]
                target = part * half + tile * LANES
                for at, value in enumerate(swap_blocks(taken, width)):
                    out_ref[:, first + at, target : target + LANES] = value


def return_rows(field, devices, rows):
    unused, frames, width, length = field.shape
    lanes = 2 * frames * width
    return pl.pallas_call(
        lambda *refs: return_kernel(devices, width, *refs),
        out_shape=jax.ShapeDtypeStruct((rows, frames, 2 * width * devices), jnp.float32),
        in_specs=[pl.BlockSpec(memory_space=pltpu.VMEM)],
        out_specs=pl.BlockSpec(memory_space=pltpu.VMEM),
        scratch_shapes=[
            pltpu.VMEM((devices, rows, lanes), jnp.float32),
            pltpu.VMEM((devices, rows, lanes), jnp.float32),
            pltpu.SemaphoreType.DMA((devices - 1,)),
            pltpu.SemaphoreType.DMA((devices - 1,)),
        ],
        compiler_params=pltpu.CompilerParams(collective_id=1, has_side_effects=True),
        name="return_rows",
    )(field.reshape(lanes, length))


def per_device(image, sens, kspace, mask):
    devices = lax.axis_size("coil")
    device = lax.axis_index("coil")
    rows_dev, frames, packed = image.shape
    coils = sens.shape[1]
    length, pairs, unused = kspace.shape
    half = packed // 2
    width = half // devices
    copies = max(1, frames // pairs)
    own_coils = max(1, pairs // frames)
    own_frames = min(frames, pairs)
    row_cos, row_sin = dft_tables(length)
    col_cos, col_sin = dft_tables(half)

    spread = sens if copies == 1 else jnp.repeat(sens, copies, axis=1)
    own_maps = lax.all_to_all(spread, "coil", split_axis=1, concat_axis=0, tiled=True)
    outgoing = pack_columns(sens, image, devices)
    incoming = lax.all_to_all(outgoing, "coil", split_axis=0, concat_axis=0, tiled=True)
    columns = jnp.transpose(incoming.reshape(length, -1))
    cut = 2 * coils * width
    maps = columns[:cut].reshape(2, coils, width, length)
    field = columns[cut:].reshape(2, frames, width, length)

    first_frame = device * pairs % frames
    mask_float = mask.astype(jnp.float32)
    local_mask = lax.dynamic_slice_in_dim(mask_float, first_frame, own_frames, 0)
    mask_pairs = jnp.tile(local_mask, (own_coils, 1))
    base_re, base_im = data_images(kspace, mask_pairs, row_cos, row_sin, col_cos, col_sin)
    base_re = base_re.reshape(length, own_coils, own_frames, half)
    base_im = base_im.reshape(length, own_coils, own_frames, half)
    own_re, own_im = (own_maps[:, :, None, :half], own_maps[:, :, None, half:])
    term_re = jnp.sum(own_re * base_re + own_im * base_im, 1)
    term_im = jnp.sum(own_re * base_im - own_im * base_re, 1)
    fits = blocked(devices, width, rows_dev, (coils, frames)) and own_frames == frames
    if fits and devices % 8 == 0:
        term = jnp.transpose(jnp.stack([term_re, term_im]), (2, 0, 3, 1))
        term = term.reshape(frames, 2, devices, width, length)
        term = jnp.transpose(term, (0, 2, 1, 3, 4)).reshape(frames, devices, 2 * width, length)
        data_term = reduce_columns(term, devices, width)
    else:
        term = jnp.transpose(jnp.stack([term_re, term_im]), (3, 0, 2, 1))
        if own_frames < frames:
            wide = jnp.zeros((half, 2, frames, length), jnp.float32)
            term = lax.dynamic_update_slice_in_dim(wide, term, first_frame, 2)
        term = term.reshape(devices, width, 2, frames, length)
        data_term = lax.psum_scatter(term, "coil", scatter_dimension=0, tiled=True)
        data_term = jnp.transpose(data_term[0], (1, 2, 0, 3))

    real, imag = projections(mask, row_cos, row_sin)
    field = iterate(field, data_term, maps, real, imag)

    if fits:
        return return_rows(field, devices, rows_dev)
    leaving = jnp.transpose(field.reshape(2 * frames * width, length))
    leaving = leaving.reshape(devices, rows_dev, 2 * frames * width)
    arrived = lax.all_to_all(leaving, "coil", split_axis=0, concat_axis=0, tiled=True)
    arrived = arrived.reshape(devices, rows_dev, 2, frames, width)
    return jnp.transpose(arrived, (1, 3, 2, 0, 4)).reshape(rows_dev, frames, packed)


def solution(mesh):
    return jax.shard_map(
        per_device,
        mesh=mesh,
        in_specs=(
            P(("plane", "coil"), None, None),
            P(("plane", "coil"), None, None),
            P("plane", "coil", None),
            P(),
        ),
        out_specs=P(("plane", "coil"), None, None),
        check_vma=False,
    )
```

```python
import jax
import jax.numpy as jnp
from jax import lax
from jax.experimental import pallas as pl
from jax.experimental.pallas import tpu as pltpu
from jax.sharding import PartitionSpec as P

OUTER = 2
INNER = 2

step_size = 0.5
tv_weight = 0.1
dual_step = 1.25
high = lax.Precision.HIGH


def contract(spec, *operands):
    return jnp.einsum(spec, *operands, precision=high, preferred_element_type=jnp.float32)


def dft_tables(length):
    index = lax.iota(jnp.int32, length)
    product = index[:, None] * index[None, :] % length
    angle = 2.0 * jnp.pi / length * product.astype(jnp.float32)
    scale = 1.0 / jnp.sqrt(jnp.float32(length))
    return (jnp.cos(angle) * scale, -jnp.sin(angle) * scale)


def column_matrix(cos_part, sin_part):
    upper = jnp.concatenate([cos_part, sin_part], 1)
    lower = jnp.concatenate([-sin_part, cos_part], 1)
    return jnp.concatenate([upper, lower], 0)


def projections(mask, row_cos, row_sin):
    weights = mask.astype(jnp.float32)
    wide = jnp.concatenate([row_cos, row_sin], 1)
    cos_rows = weights[:, :, None] * row_cos[None]
    sin_rows = weights[:, :, None] * row_sin[None]
    from_cos = contract("fka,ky->fay", cos_rows, wide)
    from_sin = contract("fka,ky->fay", sin_rows, wide)
    length = row_cos.shape[0]
    real = from_cos[..., :length] + from_sin[..., length:]
    imag = from_cos[..., length:] - from_sin[..., :length]
    return (real, imag)


def to_columns(field, devices):
    rows, count, packed = field.shape
    width = packed // 2 // devices
    parts = field.reshape(rows, count, 2, devices, width)
    return jnp.transpose(parts, (3, 0, 2, 1, 4)).reshape(devices, rows, 2 * count * width)


def divergence(dual_time, dual_rows):
    time_axis, row_axis = 1, 3
    zero_time = jnp.zeros_like(dual_time[:, :1])
    zero_rows = jnp.zeros_like(dual_rows[..., :1])
    head_time = dual_time[:, :-1]
    head_rows = dual_rows[..., :-1]
    from_time = jnp.concatenate([zero_time, head_time], time_axis) - jnp.concatenate(
        [head_time, zero_time], time_axis
    )
    from_rows = jnp.concatenate([zero_rows, head_rows], row_axis) - jnp.concatenate(
        [head_rows, zero_rows], row_axis
    )
    return from_time + from_rows


def forward_diff(field):
    diff_time = jnp.concatenate(
        [field[:, 1:] - field[:, :-1], jnp.zeros_like(field[:, :1])], 1
    )
    diff_rows = jnp.concatenate(
        [field[..., 1:] - field[..., :-1], jnp.zeros_like(field[..., :1])], 3
    )
    return (diff_time, diff_rows)


def denoise(target):
    dual_time = jnp.zeros_like(target)
    dual_rows = jnp.zeros_like(target)
    for repeat in range(INNER):
        primal = target
        if repeat:
            primal = target - tv_weight * divergence(dual_time, dual_rows)
        diff_time, diff_rows = forward_diff(primal)
        dual_time = jnp.clip(dual_time + dual_step * diff_time, -1.0, 1.0)
        dual_rows = jnp.clip(dual_rows + dual_step * diff_rows, -1.0, 1.0)
    return target - tv_weight * divergence(dual_time, dual_rows)


def iterate(field, data_term, maps, real, imag):
    maps_re, maps_im = (maps[0][None], maps[1][None])
    for sweep in range(OUTER):
        now_re, now_im = (field[0][:, None], field[1][:, None])
        seen_re = maps_re * now_re - maps_im * now_im
        seen_im = maps_re * now_im + maps_im * now_re
        kept_re = contract("fczy,fky->fczk", seen_re, real) - contract(
            "fczy,fky->fczk", seen_im, imag
        )
        kept_im = contract("fczy,fky->fczk", seen_re, imag) + contract(
            "fczy,fky->fczk", seen_im, real
        )
        grad_re = jnp.sum(maps_re * kept_re + maps_im * kept_im, 1)
        grad_im = jnp.sum(maps_re * kept_im - maps_im * kept_re, 1)
        gradient = jnp.stack([grad_re, grad_im]) - data_term
        field = denoise(field - step_size * gradient)
    return field


def data_images(kspace, mask_pairs, row_cos, row_sin, col_cos, col_sin):
    masked = jnp.transpose(mask_pairs)[:, :, None] * kspace
    mid = contract("kpz,zw->kpw", masked, column_matrix(col_cos, -col_sin))
    half = kspace.shape[-1] // 2
    from_cos = contract("ky,kpz->ypz", row_cos, mid)
    from_sin = contract("ky,kpz->ypz", row_sin, mid)
    real = from_cos[..., :half] + from_sin[..., half:]
    imag = from_cos[..., half:] - from_sin[..., :half]
    return (real, imag)


LANES = 128
SUBLANES = 8


def swap_blocks(values, width):
    count = len(values)
    block = lax.broadcasted_iota(jnp.int32, values[0].shape, 1) // width
    step = count // 2
    while step:
        lower = block // step % 2 == 0
        shift = step * width
        values = list(values)
        for at in range(count):
            if at // step % 2 == 0:
                near, far = (values[at], values[at + step])
                values[at] = jnp.where(lower, near, pltpu.roll(far, shift, 1))
                values[at + step] = jnp.where(lower, pltpu.roll(near, LANES - shift, 1), far)
        step //= 2
    return values


def blocked(devices, width, rows, counts):
    group = LANES // width
    fits = LANES % width == 0 and width % SUBLANES == 0 and rows % SUBLANES == 0
    return fits and devices % group == 0 and all(count % group == 0 for count in counts)


def pack_kernel(devices, width, sens_ref, image_ref, out_ref):
    group = LANES // width
    half = devices * width
    start = 0
    for source in (sens_ref, image_ref):
        count = source.shape[1]
        for part in range(2):
            for tile in range(half // LANES):
                lane = part * half + tile * LANES
                for first in range(0, count, group):
                    taken = [source[:, first + at, lane : lane + LANES] for at in range(group)]
                    target = start + (part * count + first) * width
                    for at, value in enumerate(swap_blocks(taken, width)):
                        out_ref[tile * group + at, :, target : target + LANES] = value
        start += 2 * count * width


def pack_columns(sens, image, devices):
    rows, coils, packed = sens.shape
    frames = image.shape[1]
    width = packed // 2 // devices
    if not blocked(devices, width, rows, (coils, frames)):
        return jnp.concatenate([to_columns(sens, devices), to_columns(image, devices)], 2)
    return pl.pallas_call(
        lambda *refs: pack_kernel(devices, width, *refs),
        out_shape=jax.ShapeDtypeStruct((devices, rows, 2 * (coils + frames) * width), jnp.float32),
        in_specs=[pl.BlockSpec(memory_space=pltpu.VMEM)] * 2,
        out_specs=pl.BlockSpec(memory_space=pltpu.VMEM),
        name="pack_columns",
    )(sens, image)


def greet(peers):
    barrier = pltpu.get_barrier_semaphore()
    for peer in peers:
        pl.semaphore_signal(barrier, 1, device_id={"coil": peer}, device_id_type=MESH)
    pl.semaphore_wait(barrier, len(peers))


MESH = pl.DeviceIdType.MESH


def reduce_kernel(
    devices, base_ref, maps_ref, out_ref, term_ref, got_a, sum_a, got_b, sum_b, got_c, send_sem, recv_sem
):
    coils, frames, unused, packed = base_ref.shape
    half = packed // 2
    width = out_ref.shape[2]
    ranks = devices // 4
    me = lax.axis_index("coil")
    core = me % 2
    side = me // 2 % 2
    rank = me // 4
    core_peer = me + 1 - 2 * core
    side_peer = me + 2 - 4 * side
    rank_peers = [(me + 4 * hop) % devices for hop in range(1, ranks)]
    greet([core_peer, side_peer] + rank_peers)

    def copy_to(source, target, frame, slot, peer):
        return pltpu.make_async_remote_copy(
            src_ref=source,
            dst_ref=target,
            send_sem=send_sem.at[frame, slot],
            recv_sem=recv_sem.at[frame, slot],
            device_id={"coil": peer},
            device_id_type=MESH,
        )

    def core_copy(frame):
        return copy_to(term_ref.at[frame, :, :, 1 - core], got_a.at[frame], frame, 0, core_peer)

    def side_copy(frame):
        return copy_to(sum_a.at[frame, :, 1 - side], got_b.at[frame], frame, 1, side_peer)

    def rank_copy(frame, hop):
        return copy_to(
            sum_b.at[frame, (rank + hop) % ranks],
            got_c.at[frame, hop - 1],
            frame,
            1 + hop,
            rank_peers[hop - 1],
        )

    def weigh(frame):
        real, imag = (0.0, 0.0)
        for coil in range(coils):
            base_re, base_im = (base_ref[coil, frame, :, :half], base_ref[coil, frame, :, half:])
            maps_re, maps_im = (maps_ref[coil, :, :half], maps_ref[coil, :, half:])
            real = real + maps_re * base_re + maps_im * base_im
            imag = imag + maps_re * base_im - maps_im * base_re
        shape = term_ref.shape[1:4] + (width, length)
        term_ref[frame, :, :, :, :width] = jnp.transpose(real).reshape(shape)
        term_ref[frame, :, :, :, width:] = jnp.transpose(imag).reshape(shape)

    length = base_ref.shape[2]
    for turn in range(frames + 3):
        if turn < frames:
            weigh(turn)
            core_copy(turn).start()
        if 0 <= turn - 1 < frames:
            frame = turn - 1
            core_copy(frame).wait()
            sum_a[frame] = term_ref[frame, :, :, core] + got_a[frame]
            side_copy(frame).start()
        if 0 <= turn - 2 < frames:
            frame = turn - 2
            side_copy(frame).wait()
            sum_b[frame] = sum_a[frame, :, side] + got_b[frame]
            for hop in range(1, ranks):
                rank_copy(frame, hop).start()
        if turn - 3 >= 0:
            frame = turn - 3
            total = sum_b[frame, rank]
            for hop in range(1, ranks):
                rank_copy(frame, hop).wait()
                total = total + got_c[frame, hop - 1]
            out_ref[0, frame] = total[:width]
            out_ref[1, frame] = total[width:]


def reduce_columns(base, own_maps, devices, width):
    unused, frames, length, unused = base.shape
    ranks = devices // 4
    return pl.pallas_call(
        lambda *refs: reduce_kernel(devices, *refs),
        out_shape=jax.ShapeDtypeStruct((2, frames, width, length), jnp.float32),
        in_specs=[pl.BlockSpec(memory_space=pltpu.VMEM)] * 2,
        out_specs=pl.BlockSpec(memory_space=pltpu.VMEM),
        scratch_shapes=[
            pltpu.VMEM((frames, ranks, 2, 2, 2 * width, length), jnp.float32),
            pltpu.VMEM((frames, ranks, 2, 2 * width, length), jnp.float32),
            pltpu.VMEM((frames, ranks, 2, 2 * width, length), jnp.float32),
            pltpu.VMEM((frames, ranks, 2 * width, length), jnp.float32),
            pltpu.VMEM((frames, ranks, 2 * width, length), jnp.float32),
            pltpu.VMEM((frames, ranks - 1, 2 * width, length), jnp.float32),
            pltpu.SemaphoreType.DMA((frames, ranks + 1)),
            pltpu.SemaphoreType.DMA((frames, ranks + 1)),
        ],
        compiler_params=pltpu.CompilerParams(collective_id=0, has_side_effects=True),
        name="reduce_columns",
    )(base, own_maps)


def return_kernel(devices, width, field_ref, out_ref, ready, landed, send_sem, recv_sem):
    rows, frames, unused = out_ref.shape
    group = LANES // width
    half = devices * width
    me = lax.axis_index("coil")
    peers = [(me + hop) % devices for hop in range(1, devices)]
    turned = jnp.transpose(field_ref[...])
    ready[...] = turned.reshape(devices, rows, turned.shape[1])
    greet(peers)
    copies = []
    for hop in range(1, devices):
        copies.append(
            pltpu.make_async_remote_copy(
                src_ref=ready.at[peers[hop - 1]],
                dst_ref=landed.at[me],
                send_sem=send_sem.at[hop - 1],
                recv_sem=recv_sem.at[hop - 1],
                device_id={"coil": peers[hop - 1]},
                device_id_type=MESH,
            )
        )
        copies[-1].start()
    landed[me] = ready[me]
    for copy in copies:
        copy.wait()
    for part in range(2):
        for first in range(0, frames, group):
            lane = (part * frames + first) * width
            for tile in range(devices // group):
                taken = [landed[tile * group + at, :, lane : lane + LANES] for at in range(group)]
                target = part * half + tile * LANES
                for at, value in enumerate(swap_blocks(taken, width)):
                    out_ref[:, first + at, target : target + LANES] = value


def return_rows(field, devices, rows):
    unused, frames, width, length = field.shape
    lanes = 2 * frames * width
    return pl.pallas_call(
        lambda *refs: return_kernel(devices, width, *refs),
        out_shape=jax.ShapeDtypeStruct((rows, frames, 2 * width * devices), jnp.float32),
        in_specs=[pl.BlockSpec(memory_space=pltpu.VMEM)],
        out_specs=pl.BlockSpec(memory_space=pltpu.VMEM),
        scratch_shapes=[
            pltpu.VMEM((devices, rows, lanes), jnp.float32),
            pltpu.VMEM((devices, rows, lanes), jnp.float32),
            pltpu.SemaphoreType.DMA((devices - 1,)),
            pltpu.SemaphoreType.DMA((devices - 1,)),
        ],
        compiler_params=pltpu.CompilerParams(collective_id=1, has_side_effects=True),
        name="return_rows",
    )(field.reshape(lanes, length))


def split(value):
    top = value.astype(jnp.bfloat16)
    return (top, (value - top.astype(jnp.float32)).astype(jnp.bfloat16))


def narrow(value):
    top = lax.reduce_precision(value, 8, 7)
    return (top.astype(jnp.bfloat16), (value - top).astype(jnp.bfloat16))


def dot3(left, right):
    def one(a, b):
        return jnp.dot(a, b, preferred_element_type=jnp.float32)

    return one(left[1], right[0]) + one(left[0], right[1]) + one(left[0], right[0])


def base_kernel(kspace_ref, mask_ref, row_top, row_low, col_top, col_low, out_ref):
    length, frames, packed = kspace_ref.shape
    half = packed // 2
    rows = (row_top[...], row_low[...])
    cols = (col_top[...], col_low[...])
    for frame in range(frames):
        masked = kspace_ref[:, frame, :] * mask_ref[:, frame : frame + 1]
        mid = dot3(split(masked), cols)
        both = dot3(rows, split(mid))
        real = both[:length, :half] + both[length:, half:]
        imag = both[:length, half:] - both[length:, :half]
        out_ref[0, frame, :, :half] = real
        out_ref[0, frame, :, half:] = imag


def base_images(kspace, mask, row_cos, row_sin, col_cos, col_sin):
    length, pairs, packed = kspace.shape
    frames = mask.shape[0]
    coils = pairs // frames
    rows = narrow(jnp.concatenate([row_cos, row_sin], 0))
    cols = narrow(column_matrix(col_cos, -col_sin))
    whole = pl.BlockSpec(memory_space=pltpu.VMEM)
    macs = pairs * 2 * length * packed * packed * 3
    return pl.pallas_call(
        base_kernel,
        grid=(coils,),
        out_shape=jax.ShapeDtypeStruct((coils, frames, length, packed), jnp.float32),
        in_specs=[pl.BlockSpec((length, frames, packed), lambda coil: (0, coil, 0))] + [whole] * 5,
        out_specs=pl.BlockSpec((1, frames, length, packed), lambda coil: (coil, 0, 0, 0)),
        cost_estimate=pl.CostEstimate(
            flops=2 * macs, bytes_accessed=2 * kspace.size * 4, transcendentals=0
        ),
        name="base_images",
    )(kspace, jnp.transpose(mask), *rows, *cols)


def per_device(image, sens, kspace, mask):
    devices = lax.axis_size("coil")
    device = lax.axis_index("coil")
    rows_dev, frames, packed = image.shape
    coils = sens.shape[1]
    length, pairs, unused = kspace.shape
    half = packed // 2
    width = half // devices
    copies = max(1, frames // pairs)
    own_coils = max(1, pairs // frames)
    own_frames = min(frames, pairs)
    row_cos, row_sin = dft_tables(length)
    col_cos, col_sin = dft_tables(half)

    spread = sens if copies == 1 else jnp.repeat(sens, copies, axis=1)
    own_maps = lax.all_to_all(spread, "coil", split_axis=1, concat_axis=0, tiled=True)
    outgoing = pack_columns(sens, image, devices)
    incoming = lax.all_to_all(outgoing, "coil", split_axis=0, concat_axis=0, tiled=True)
    columns = jnp.transpose(incoming.reshape(length, -1))
    cut = 2 * coils * width
    maps = columns[:cut].reshape(2, coils, width, length)
    field = columns[cut:].reshape(2, frames, width, length)

    first_frame = device * pairs % frames
    mask_float = mask.astype(jnp.float32)
    local_mask = lax.dynamic_slice_in_dim(mask_float, first_frame, own_frames, 0)
    fits = blocked(devices, width, rows_dev, (coils, frames)) and own_frames == frames
    if fits and devices % 8 == 0 and frames % SUBLANES == 0:
        base = base_images(kspace, mask_float, row_cos, row_sin, col_cos, col_sin)
        data_term = reduce_columns(base, jnp.transpose(own_maps, (1, 0, 2)), devices, width)
    else:
        mask_pairs = jnp.tile(local_mask, (own_coils, 1))
        base_re, base_im = data_images(kspace, mask_pairs, row_cos, row_sin, col_cos, col_sin)
        base_re = base_re.reshape(length, own_coils, own_frames, half)
        base_im = base_im.reshape(length, own_coils, own_frames, half)
        own_re, own_im = (own_maps[:, :, None, :half], own_maps[:, :, None, half:])
        term_re = jnp.sum(own_re * base_re + own_im * base_im, 1)
        term_im = jnp.sum(own_re * base_im - own_im * base_re, 1)
        term = jnp.transpose(jnp.stack([term_re, term_im]), (3, 0, 2, 1))
        if own_frames < frames:
            wide = jnp.zeros((half, 2, frames, length), jnp.float32)
            term = lax.dynamic_update_slice_in_dim(wide, term, first_frame, 2)
        term = term.reshape(devices, width, 2, frames, length)
        data_term = lax.psum_scatter(term, "coil", scatter_dimension=0, tiled=True)
        data_term = jnp.transpose(data_term[0], (1, 2, 0, 3))

    real, imag = projections(mask, row_cos, row_sin)
    field = iterate(field, data_term, maps, real, imag)

    if fits:
        return return_rows(field, devices, rows_dev)
    leaving = jnp.transpose(field.reshape(2 * frames * width, length))
    leaving = leaving.reshape(devices, rows_dev, 2 * frames * width)
    arrived = lax.all_to_all(leaving, "coil", split_axis=0, concat_axis=0, tiled=True)
    arrived = arrived.reshape(devices, rows_dev, 2, frames, width)
    return jnp.transpose(arrived, (1, 3, 2, 0, 4)).reshape(rows_dev, frames, packed)


def solution(mesh):
    return jax.shard_map(
        per_device,
        mesh=mesh,
        in_specs=(
            P(("plane", "coil"), None, None),
            P(("plane", "coil"), None, None),
            P("plane", "coil", None),
            P(),
        ),
        out_specs=P(("plane", "coil"), None, None),
        check_vma=False,
    )
```

```python
import jax
import jax.numpy as jnp
from jax import lax
from jax.experimental import pallas as pl
from jax.experimental.pallas import tpu as pltpu
from jax.sharding import PartitionSpec as P

OUTER = 2
INNER = 2

step_size = 0.5
tv_weight = 0.1
dual_step = 1.25
high = lax.Precision.HIGH


def contract(spec, *operands):
    return jnp.einsum(spec, *operands, precision=high, preferred_element_type=jnp.float32)


def dft_tables(length):
    index = lax.iota(jnp.int32, length)
    product = index[:, None] * index[None, :] % length
    angle = 2.0 * jnp.pi / length * product.astype(jnp.float32)
    scale = 1.0 / jnp.sqrt(jnp.float32(length))
    return (jnp.cos(angle) * scale, -jnp.sin(angle) * scale)


def column_matrix(cos_part, sin_part):
    upper = jnp.concatenate([cos_part, sin_part], 1)
    lower = jnp.concatenate([-sin_part, cos_part], 1)
    return jnp.concatenate([upper, lower], 0)


def projections(mask, row_cos, row_sin):
    weights = mask.astype(jnp.float32)
    wide = jnp.concatenate([row_cos, row_sin], 1)
    cos_rows = weights[:, :, None] * row_cos[None]
    sin_rows = weights[:, :, None] * row_sin[None]
    from_cos = contract("fka,ky->fay", cos_rows, wide)
    from_sin = contract("fka,ky->fay", sin_rows, wide)
    length = row_cos.shape[0]
    real = from_cos[..., :length] + from_sin[..., length:]
    imag = from_cos[..., length:] - from_sin[..., :length]
    return (real, imag)


def to_columns(field, devices):
    rows, count, packed = field.shape
    width = packed // 2 // devices
    parts = field.reshape(rows, count, 2, devices, width)
    return jnp.transpose(parts, (3, 0, 2, 1, 4)).reshape(devices, rows, 2 * count * width)


def divergence(dual_time, dual_rows):
    time_axis, row_axis = 1, 3
    zero_time = jnp.zeros_like(dual_time[:, :1])
    zero_rows = jnp.zeros_like(dual_rows[..., :1])
    head_time = dual_time[:, :-1]
    head_rows = dual_rows[..., :-1]
    from_time = jnp.concatenate([zero_time, head_time], time_axis) - jnp.concatenate(
        [head_time, zero_time], time_axis
    )
    from_rows = jnp.concatenate([zero_rows, head_rows], row_axis) - jnp.concatenate(
        [head_rows, zero_rows], row_axis
    )
    return from_time + from_rows


def forward_diff(field):
    diff_time = jnp.concatenate(
        [field[:, 1:] - field[:, :-1], jnp.zeros_like(field[:, :1])], 1
    )
    diff_rows = jnp.concatenate(
        [field[..., 1:] - field[..., :-1], jnp.zeros_like(field[..., :1])], 3
    )
    return (diff_time, diff_rows)


def denoise(target):
    dual_time = jnp.zeros_like(target)
    dual_rows = jnp.zeros_like(target)
    for repeat in range(INNER):
        primal = target
        if repeat:
            primal = target - tv_weight * divergence(dual_time, dual_rows)
        diff_time, diff_rows = forward_diff(primal)
        dual_time = jnp.clip(dual_time + dual_step * diff_time, -1.0, 1.0)
        dual_rows = jnp.clip(dual_rows + dual_step * diff_rows, -1.0, 1.0)
    return target - tv_weight * divergence(dual_time, dual_rows)


def iterate(field, data_term, maps, real, imag):
    maps_re, maps_im = (maps[0][None], maps[1][None])
    for sweep in range(OUTER):
        now_re, now_im = (field[0][:, None], field[1][:, None])
        seen_re = maps_re * now_re - maps_im * now_im
        seen_im = maps_re * now_im + maps_im * now_re
        kept_re = contract("fczy,fky->fczk", seen_re, real) - contract(
            "fczy,fky->fczk", seen_im, imag
        )
        kept_im = contract("fczy,fky->fczk", seen_re, imag) + contract(
            "fczy,fky->fczk", seen_im, real
        )
        grad_re = jnp.sum(maps_re * kept_re + maps_im * kept_im, 1)
        grad_im = jnp.sum(maps_re * kept_im - maps_im * kept_re, 1)
        gradient = jnp.stack([grad_re, grad_im]) - data_term
        field = denoise(field - step_size * gradient)
    return field


def data_images(kspace, mask_pairs, row_cos, row_sin, col_cos, col_sin):
    masked = jnp.transpose(mask_pairs)[:, :, None] * kspace
    mid = contract("kpz,zw->kpw", masked, column_matrix(col_cos, -col_sin))
    half = kspace.shape[-1] // 2
    from_cos = contract("ky,kpz->ypz", row_cos, mid)
    from_sin = contract("ky,kpz->ypz", row_sin, mid)
    real = from_cos[..., :half] + from_sin[..., half:]
    imag = from_cos[..., half:] - from_sin[..., :half]
    return (real, imag)


LANES = 128
SUBLANES = 8


def swap_blocks(values, width):
    count = len(values)
    block = lax.broadcasted_iota(jnp.int32, values[0].shape, 1) // width
    step = count // 2
    while step:
        lower = block // step % 2 == 0
        shift = step * width
        values = list(values)
        for at in range(count):
            if at // step % 2 == 0:
                near, far = (values[at], values[at + step])
                values[at] = jnp.where(lower, near, pltpu.roll(far, shift, 1))
                values[at + step] = jnp.where(lower, pltpu.roll(near, LANES - shift, 1), far)
        step //= 2
    return values


def blocked(devices, width, rows, counts):
    group = LANES // width
    fits = LANES % width == 0 and width % SUBLANES == 0 and rows % SUBLANES == 0
    return fits and devices % group == 0 and all(count % group == 0 for count in counts)


def pack_kernel(devices, width, sens_ref, image_ref, out_ref):
    group = LANES // width
    half = devices * width
    start = 0
    for source in (sens_ref, image_ref):
        count = source.shape[0]
        for part in range(2):
            for tile in range(half // LANES):
                lane = part * half + tile * LANES
                for first in range(0, count, group):
                    taken = [source[first + at, :, lane : lane + LANES] for at in range(group)]
                    target = start + (part * count + first) * width
                    for at, value in enumerate(swap_blocks(taken, width)):
                        out_ref[tile * group + at, :, target : target + LANES] = value
        start += 2 * count * width


def greet(peers):
    barrier = pltpu.get_barrier_semaphore()
    for peer in peers:
        pl.semaphore_signal(barrier, 1, device_id={"coil": peer}, device_id_type=MESH)
    pl.semaphore_wait(barrier, len(peers))


MESH = pl.DeviceIdType.MESH


def gather_kernel(
    devices,
    sens_ref,
    image_ref,
    kspace_ref,
    mask_ref,
    row_top,
    row_low,
    col_top,
    col_low,
    out_ref,
    columns_ref,
    data_ref,
    base_ref,
    maps_ref,
    packed_ref,
    landed_ref,
    term_ref,
    got_a,
    sum_a,
    got_b,
    sum_b,
    got_c,
    send_sem,
    recv_sem,
    maps_send,
    maps_recv,
    pack_send,
    pack_recv,
    data_sem,
):
    coils, frames, length, packed = base_ref.shape
    rows = sens_ref.shape[1]
    half = packed // 2
    width = out_ref.shape[2]
    ranks = devices // 4
    me = lax.axis_index("coil")
    core = me % 2
    side = me // 2 % 2
    rank = me // 4
    core_peer = me + 1 - 2 * core
    side_peer = me + 2 - 4 * side
    rank_peers = [(me + 4 * hop) % devices for hop in range(1, ranks)]
    peers = [(me + hop) % devices for hop in range(1, devices)]

    def data_copy(coil):
        return pltpu.make_async_copy(
            kspace_ref.at[:, pl.ds(coil * frames, frames), :], data_ref.at[coil], data_sem.at[coil]
        )

    def maps_copy(hop):
        return pltpu.make_async_remote_copy(
            src_ref=sens_ref.at[pl.ds(peers[hop - 1] * coils, coils)],
            dst_ref=maps_ref.at[:, pl.ds(pl.multiple_of(me * rows, SUBLANES), rows), :],
            send_sem=maps_send.at[hop - 1],
            recv_sem=maps_recv.at[hop - 1],
            device_id={"coil": peers[hop - 1]},
            device_id_type=MESH,
        )

    def pack_copy(hop):
        return pltpu.make_async_remote_copy(
            src_ref=packed_ref.at[peers[hop - 1]],
            dst_ref=landed_ref.at[me],
            send_sem=pack_send.at[hop - 1],
            recv_sem=pack_recv.at[hop - 1],
            device_id={"coil": peers[hop - 1]},
            device_id_type=MESH,
        )

    for coil in range(coils):
        data_copy(coil).start()
    greet(peers)
    for hop in range(1, devices):
        maps_copy(hop).start()
    pack_kernel(devices, width, sens_ref, image_ref, packed_ref)
    for hop in range(1, devices):
        pack_copy(hop).start()
    maps_ref[:, pl.ds(pl.multiple_of(me * rows, SUBLANES), rows), :] = sens_ref[
        pl.ds(me * coils, coils)
    ]
    landed_ref[me] = packed_ref[me]

    row_pair = (row_top[...], row_low[...])
    col_pair = (col_top[...], col_low[...])
    for coil in range(coils):
        data_copy(coil).wait()
        for frame in range(frames):
            masked = data_ref[coil, :, frame, :] * mask_ref[:, frame : frame + 1]
            mid = dot3(split(masked), col_pair)
            both = dot3(row_pair, split(mid))
            base_ref[coil, frame, :, :half] = both[:length, :half] + both[length:, half:]
            base_ref[coil, frame, :, half:] = both[:length, half:] - both[length:, :half]
    for hop in range(1, devices):
        maps_copy(hop).wait()

    def copy_to(source, target, frame, slot, peer):
        return pltpu.make_async_remote_copy(
            src_ref=source,
            dst_ref=target,
            send_sem=send_sem.at[frame, slot],
            recv_sem=recv_sem.at[frame, slot],
            device_id={"coil": peer},
            device_id_type=MESH,
        )

    def core_copy(frame):
        return copy_to(term_ref.at[frame, :, :, 1 - core], got_a.at[frame], frame, 0, core_peer)

    def side_copy(frame):
        return copy_to(sum_a.at[frame, :, 1 - side], got_b.at[frame], frame, 1, side_peer)

    def rank_copy(frame, hop):
        return copy_to(
            sum_b.at[frame, (rank + hop) % ranks],
            got_c.at[frame, hop - 1],
            frame,
            1 + hop,
            rank_peers[hop - 1],
        )

    def weigh(frame):
        real, imag = (0.0, 0.0)
        for coil in range(coils):
            base_re, base_im = (base_ref[coil, frame, :, :half], base_ref[coil, frame, :, half:])
            maps_re, maps_im = (maps_ref[coil, :, :half], maps_ref[coil, :, half:])
            real = real + maps_re * base_re + maps_im * base_im
            imag = imag + maps_re * base_im - maps_im * base_re
        shape = term_ref.shape[1:4] + (width, length)
        term_ref[frame, :, :, :, :width] = jnp.transpose(real).reshape(shape)
        term_ref[frame, :, :, :, width:] = jnp.transpose(imag).reshape(shape)

    for turn in range(frames + 3):
        if turn < frames:
            weigh(turn)
            core_copy(turn).start()
        if 0 <= turn - 1 < frames:
            frame = turn - 1
            core_copy(frame).wait()
            sum_a[frame] = term_ref[frame, :, :, core] + got_a[frame]
            side_copy(frame).start()
        if 0 <= turn - 2 < frames:
            frame = turn - 2
            side_copy(frame).wait()
            sum_b[frame] = sum_a[frame, :, side] + got_b[frame]
            for hop in range(1, ranks):
                rank_copy(frame, hop).start()
        if turn - 3 >= 0:
            frame = turn - 3
            total = sum_b[frame, rank]
            for hop in range(1, ranks):
                rank_copy(frame, hop).wait()
                total = total + got_c[frame, hop - 1]
            out_ref[0, frame] = total[:width]
            out_ref[1, frame] = total[width:]

    for hop in range(1, devices):
        pack_copy(hop).wait()
    columns_ref[...] = jnp.transpose(landed_ref[...].reshape(length, landed_ref.shape[2]))


def gather(image, sens, kspace, mask, devices, tables):
    rows, frames, packed = image.shape
    length, pairs, unused = kspace.shape
    coils = pairs // frames
    ranks = devices // 4
    width = packed // 2 // devices
    lanes = 2 * (sens.shape[1] + frames) * width
    row_cos, row_sin, col_cos, col_sin = tables
    row_pair = narrow(jnp.concatenate([row_cos, row_sin], 0))
    col_pair = narrow(column_matrix(col_cos, -col_sin))
    block = (2 * width, length)
    whole = pl.BlockSpec(memory_space=pltpu.VMEM)

    def held(*shape):
        return pltpu.VMEM(shape, jnp.float32)

    dma = pltpu.SemaphoreType.DMA
    return pl.pallas_call(
        lambda *refs: gather_kernel(devices, *refs),
        out_shape=(
            jax.ShapeDtypeStruct((2, frames, width, length), jnp.float32),
            jax.ShapeDtypeStruct((lanes, length), jnp.float32),
        ),
        in_specs=[whole] * 2 + [pl.BlockSpec(memory_space=pl.ANY)] + [whole] * 5,
        out_specs=(whole, whole),
        scratch_shapes=[
            held(coils, length, frames, packed),
            held(coils, frames, length, packed),
            held(coils, length, packed),
            held(devices, rows, lanes),
            held(devices, rows, lanes),
            held(frames, ranks, 2, 2, *block),
            held(frames, ranks, 2, *block),
            held(frames, ranks, 2, *block),
            held(frames, ranks, *block),
            held(frames, ranks, *block),
            held(frames, ranks - 1, *block),
            dma((frames, ranks + 1)),
            dma((frames, ranks + 1)),
            dma((devices - 1,)),
            dma((devices - 1,)),
            dma((devices - 1,)),
            dma((devices - 1,)),
            dma((coils,)),
        ],
        compiler_params=pltpu.CompilerParams(
            collective_id=0, has_side_effects=True, vmem_limit_bytes=60 * 1024 * 1024
        ),
        name="gather_reduce",
    )(
        jnp.transpose(sens, (1, 0, 2)),
        jnp.transpose(image, (1, 0, 2)),
        kspace,
        jnp.transpose(mask),
        *row_pair,
        *col_pair,
    )


def return_kernel(devices, width, field_ref, out_ref, ready, landed, send_sem, recv_sem):
    rows, frames, unused = out_ref.shape
    group = LANES // width
    half = devices * width
    me = lax.axis_index("coil")
    peers = [(me + hop) % devices for hop in range(1, devices)]
    turned = jnp.transpose(field_ref[...])
    ready[...] = turned.reshape(devices, rows, turned.shape[1])
    greet(peers)
    copies = []
    for hop in range(1, devices):
        copies.append(
            pltpu.make_async_remote_copy(
                src_ref=ready.at[peers[hop - 1]],
                dst_ref=landed.at[me],
                send_sem=send_sem.at[hop - 1],
                recv_sem=recv_sem.at[hop - 1],
                device_id={"coil": peers[hop - 1]},
                device_id_type=MESH,
            )
        )
        copies[-1].start()
    landed[me] = ready[me]
    for copy in copies:
        copy.wait()
    for part in range(2):
        for first in range(0, frames, group):
            lane = (part * frames + first) * width
            for tile in range(devices // group):
                taken = [landed[tile * group + at, :, lane : lane + LANES] for at in range(group)]
                target = part * half + tile * LANES
                for at, value in enumerate(swap_blocks(taken, width)):
                    out_ref[:, first + at, target : target + LANES] = value


def return_rows(field, devices, rows):
    unused, frames, width, length = field.shape
    lanes = 2 * frames * width
    return pl.pallas_call(
        lambda *refs: return_kernel(devices, width, *refs),
        out_shape=jax.ShapeDtypeStruct((rows, frames, 2 * width * devices), jnp.float32),
        in_specs=[pl.BlockSpec(memory_space=pltpu.VMEM)],
        out_specs=pl.BlockSpec(memory_space=pltpu.VMEM),
        scratch_shapes=[
            pltpu.VMEM((devices, rows, lanes), jnp.float32),
            pltpu.VMEM((devices, rows, lanes), jnp.float32),
            pltpu.SemaphoreType.DMA((devices - 1,)),
            pltpu.SemaphoreType.DMA((devices - 1,)),
        ],
        compiler_params=pltpu.CompilerParams(collective_id=1, has_side_effects=True),
        name="return_rows",
    )(field.reshape(lanes, length))


def split(value):
    top = value.astype(jnp.bfloat16)
    return (top, (value - top.astype(jnp.float32)).astype(jnp.bfloat16))


def narrow(value):
    top = lax.reduce_precision(value, 8, 7)
    return (top.astype(jnp.bfloat16), (value - top).astype(jnp.bfloat16))


def dot3(left, right):
    def one(a, b):
        return jnp.dot(a, b, preferred_element_type=jnp.float32)

    return one(left[1], right[0]) + one(left[0], right[1]) + one(left[0], right[0])


def per_device(image, sens, kspace, mask):
    devices = lax.axis_size("coil")
    device = lax.axis_index("coil")
    rows_dev, frames, packed = image.shape
    coils = sens.shape[1]
    length, pairs, unused = kspace.shape
    half = packed // 2
    width = half // devices
    copies = max(1, frames // pairs)
    own_coils = max(1, pairs // frames)
    own_frames = min(frames, pairs)
    row_cos, row_sin = dft_tables(length)
    col_cos, col_sin = dft_tables(half)

    mask_float = mask.astype(jnp.float32)
    fits = blocked(devices, width, rows_dev, (coils, frames)) and own_frames == frames
    fits = fits and devices % 8 == 0 and frames % SUBLANES == 0
    if fits:
        tables = (row_cos, row_sin, col_cos, col_sin)
        data_term, columns = gather(image, sens, kspace, mask_float, devices, tables)
    else:
        spread = sens if copies == 1 else jnp.repeat(sens, copies, axis=1)
        own_maps = lax.all_to_all(spread, "coil", split_axis=1, concat_axis=0, tiled=True)
        outgoing = jnp.concatenate([to_columns(sens, devices), to_columns(image, devices)], 2)
        incoming = lax.all_to_all(outgoing, "coil", split_axis=0, concat_axis=0, tiled=True)
        columns = jnp.transpose(incoming.reshape(length, -1))
        first_frame = device * pairs % frames
        local_mask = lax.dynamic_slice_in_dim(mask_float, first_frame, own_frames, 0)
        mask_pairs = jnp.tile(local_mask, (own_coils, 1))
        base_re, base_im = data_images(kspace, mask_pairs, row_cos, row_sin, col_cos, col_sin)
        base_re = base_re.reshape(length, own_coils, own_frames, half)
        base_im = base_im.reshape(length, own_coils, own_frames, half)
        own_re, own_im = (own_maps[:, :, None, :half], own_maps[:, :, None, half:])
        term_re = jnp.sum(own_re * base_re + own_im * base_im, 1)
        term_im = jnp.sum(own_re * base_im - own_im * base_re, 1)
        term = jnp.transpose(jnp.stack([term_re, term_im]), (3, 0, 2, 1))
        if own_frames < frames:
            wide = jnp.zeros((half, 2, frames, length), jnp.float32)
            term = lax.dynamic_update_slice_in_dim(wide, term, first_frame, 2)
        term = term.reshape(devices, width, 2, frames, length)
        data_term = lax.psum_scatter(term, "coil", scatter_dimension=0, tiled=True)
        data_term = jnp.transpose(data_term[0], (1, 2, 0, 3))

    cut = 2 * coils * width
    maps = columns[:cut].reshape(2, coils, width, length)
    field = columns[cut:].reshape(2, frames, width, length)
    real, imag = projections(mask, row_cos, row_sin)
    field = iterate(field, data_term, maps, real, imag)

    if fits:
        return return_rows(field, devices, rows_dev)
    leaving = jnp.transpose(field.reshape(2 * frames * width, length))
    leaving = leaving.reshape(devices, rows_dev, 2 * frames * width)
    arrived = lax.all_to_all(leaving, "coil", split_axis=0, concat_axis=0, tiled=True)
    arrived = arrived.reshape(devices, rows_dev, 2, frames, width)
    return jnp.transpose(arrived, (1, 3, 2, 0, 4)).reshape(rows_dev, frames, packed)


def solution(mesh):
    return jax.shard_map(
        per_device,
        mesh=mesh,
        in_specs=(
            P(("plane", "coil"), None, None),
            P(("plane", "coil"), None, None),
            P("plane", "coil", None),
            P(),
        ),
        out_specs=P(("plane", "coil"), None, None),
        check_vma=False,
    )
```

```python
import jax
import jax.numpy as jnp
from jax import lax
from jax.experimental import pallas as pl
from jax.experimental.pallas import tpu as pltpu
from jax.sharding import PartitionSpec as P

OUTER = 2
INNER = 2

step_size = 0.5
tv_weight = 0.1
dual_step = 1.25
high = lax.Precision.HIGH


def contract(spec, *operands):
    return jnp.einsum(spec, *operands, precision=high, preferred_element_type=jnp.float32)


def dft_tables(length):
    index = lax.iota(jnp.int32, length)
    product = index[:, None] * index[None, :] % length
    angle = 2.0 * jnp.pi / length * product.astype(jnp.float32)
    scale = 1.0 / jnp.sqrt(jnp.float32(length))
    return (jnp.cos(angle) * scale, -jnp.sin(angle) * scale)


def column_matrix(cos_part, sin_part):
    upper = jnp.concatenate([cos_part, sin_part], 1)
    lower = jnp.concatenate([-sin_part, cos_part], 1)
    return jnp.concatenate([upper, lower], 0)


def projections(mask, row_cos, row_sin):
    weights = mask.astype(jnp.float32)
    wide = jnp.concatenate([row_cos, row_sin], 1)
    cos_rows = weights[:, :, None] * row_cos[None]
    sin_rows = weights[:, :, None] * row_sin[None]
    from_cos = contract("fka,ky->fay", cos_rows, wide)
    from_sin = contract("fka,ky->fay", sin_rows, wide)
    length = row_cos.shape[0]
    real = from_cos[..., :length] + from_sin[..., length:]
    imag = from_cos[..., length:] - from_sin[..., :length]
    return (real, imag)


def to_columns(field, devices):
    rows, count, packed = field.shape
    width = packed // 2 // devices
    parts = field.reshape(rows, count, 2, devices, width)
    return jnp.transpose(parts, (3, 0, 2, 1, 4)).reshape(devices, rows, 2 * count * width)


def divergence(dual_time, dual_rows):
    time_axis, row_axis = 1, 3
    zero_time = jnp.zeros_like(dual_time[:, :1])
    zero_rows = jnp.zeros_like(dual_rows[..., :1])
    head_time = dual_time[:, :-1]
    head_rows = dual_rows[..., :-1]
    from_time = jnp.concatenate([zero_time, head_time], time_axis) - jnp.concatenate(
        [head_time, zero_time], time_axis
    )
    from_rows = jnp.concatenate([zero_rows, head_rows], row_axis) - jnp.concatenate(
        [head_rows, zero_rows], row_axis
    )
    return from_time + from_rows


def forward_diff(field):
    diff_time = jnp.concatenate(
        [field[:, 1:] - field[:, :-1], jnp.zeros_like(field[:, :1])], 1
    )
    diff_rows = jnp.concatenate(
        [field[..., 1:] - field[..., :-1], jnp.zeros_like(field[..., :1])], 3
    )
    return (diff_time, diff_rows)


def denoise(target):
    dual_time = jnp.zeros_like(target)
    dual_rows = jnp.zeros_like(target)
    for repeat in range(INNER):
        primal = target
        if repeat:
            primal = target - tv_weight * divergence(dual_time, dual_rows)
        diff_time, diff_rows = forward_diff(primal)
        dual_time = jnp.clip(dual_time + dual_step * diff_time, -1.0, 1.0)
        dual_rows = jnp.clip(dual_rows + dual_step * diff_rows, -1.0, 1.0)
    return target - tv_weight * divergence(dual_time, dual_rows)


def iterate(field, data_term, maps, real, imag, opening):
    maps_re, maps_im = (maps[0][None], maps[1][None])
    for sweep in range(OUTER):
        if sweep == 0 and opening is not None:
            field = denoise(field - step_size * (opening - data_term))
            continue
        now_re, now_im = (field[0][:, None], field[1][:, None])
        seen_re = maps_re * now_re - maps_im * now_im
        seen_im = maps_re * now_im + maps_im * now_re
        kept_re = contract("fczy,fky->fczk", seen_re, real) - contract(
            "fczy,fky->fczk", seen_im, imag
        )
        kept_im = contract("fczy,fky->fczk", seen_re, imag) + contract(
            "fczy,fky->fczk", seen_im, real
        )
        grad_re = jnp.sum(maps_re * kept_re + maps_im * kept_im, 1)
        grad_im = jnp.sum(maps_re * kept_im - maps_im * kept_re, 1)
        gradient = jnp.stack([grad_re, grad_im]) - data_term
        field = denoise(field - step_size * gradient)
    return field


def data_images(kspace, mask_pairs, row_cos, row_sin, col_cos, col_sin):
    masked = jnp.transpose(mask_pairs)[:, :, None] * kspace
    mid = contract("kpz,zw->kpw", masked, column_matrix(col_cos, -col_sin))
    half = kspace.shape[-1] // 2
    from_cos = contract("ky,kpz->ypz", row_cos, mid)
    from_sin = contract("ky,kpz->ypz", row_sin, mid)
    real = from_cos[..., :half] + from_sin[..., half:]
    imag = from_cos[..., half:] - from_sin[..., :half]
    return (real, imag)


LANES = 128
SUBLANES = 8


def swap_blocks(values, width):
    count = len(values)
    block = lax.broadcasted_iota(jnp.int32, values[0].shape, 1) // width
    step = count // 2
    while step:
        lower = block // step % 2 == 0
        shift = step * width
        values = list(values)
        for at in range(count):
            if at // step % 2 == 0:
                near, far = (values[at], values[at + step])
                values[at] = jnp.where(lower, near, pltpu.roll(far, shift, 1))
                values[at + step] = jnp.where(lower, pltpu.roll(near, LANES - shift, 1), far)
        step //= 2
    return values


def blocked(devices, width, rows, counts):
    group = LANES // width
    fits = LANES % width == 0 and width % SUBLANES == 0 and rows % SUBLANES == 0
    return fits and devices % group == 0 and all(count % group == 0 for count in counts)


def pack_kernel(devices, width, sens_ref, image_ref, out_ref):
    group = LANES // width
    half = devices * width
    start = 0
    for source in (sens_ref, image_ref):
        count = source.shape[0]
        for part in range(2):
            for tile in range(half // LANES):
                lane = part * half + tile * LANES
                for first in range(0, count, group):
                    taken = [source[first + at, :, lane : lane + LANES] for at in range(group)]
                    target = start + (part * count + first) * width
                    for at, value in enumerate(swap_blocks(taken, width)):
                        out_ref[tile * group + at, :, target : target + LANES] = value
        start += 2 * count * width


def greet(peers):
    barrier = pltpu.get_barrier_semaphore()
    for peer in peers:
        pl.semaphore_signal(barrier, 1, device_id={"coil": peer}, device_id_type=MESH)
    pl.semaphore_wait(barrier, len(peers))


MESH = pl.DeviceIdType.MESH


def gather_kernel(
    devices,
    sens_ref,
    image_ref,
    kspace_ref,
    mask_ref,
    row_top,
    row_low,
    col_top,
    col_low,
    real_ref,
    imag_ref,
    out_ref,
    columns_ref,
    grad_ref,
    data_ref,
    base_ref,
    maps_ref,
    packed_ref,
    landed_ref,
    term_ref,
    got_a,
    sum_a,
    got_b,
    sum_b,
    got_c,
    send_sem,
    recv_sem,
    maps_send,
    maps_recv,
    pack_send,
    pack_recv,
    data_sem,
):
    coils, frames, length, packed = base_ref.shape
    rows = sens_ref.shape[1]
    half = packed // 2
    width = out_ref.shape[2]
    ranks = devices // 4
    me = lax.axis_index("coil")
    core = me % 2
    side = me // 2 % 2
    rank = me // 4
    core_peer = me + 1 - 2 * core
    side_peer = me + 2 - 4 * side
    rank_peers = [(me + 4 * hop) % devices for hop in range(1, ranks)]
    peers = [(me + hop) % devices for hop in range(1, devices)]

    def data_copy(coil):
        return pltpu.make_async_copy(
            kspace_ref.at[:, pl.ds(coil * frames, frames), :], data_ref.at[coil], data_sem.at[coil]
        )

    def maps_copy(hop):
        return pltpu.make_async_remote_copy(
            src_ref=sens_ref.at[pl.ds(peers[hop - 1] * coils, coils)],
            dst_ref=maps_ref.at[:, pl.ds(pl.multiple_of(me * rows, SUBLANES), rows), :],
            send_sem=maps_send.at[hop - 1],
            recv_sem=maps_recv.at[hop - 1],
            device_id={"coil": peers[hop - 1]},
            device_id_type=MESH,
        )

    def pack_copy(hop):
        return pltpu.make_async_remote_copy(
            src_ref=packed_ref.at[peers[hop - 1]],
            dst_ref=landed_ref.at[me],
            send_sem=pack_send.at[hop - 1],
            recv_sem=pack_recv.at[hop - 1],
            device_id={"coil": peers[hop - 1]},
            device_id_type=MESH,
        )

    for coil in range(coils):
        data_copy(coil).start()
    greet(peers)
    for hop in range(1, devices):
        maps_copy(hop).start()
    pack_kernel(devices, width, sens_ref, image_ref, packed_ref)
    for hop in range(1, devices):
        pack_copy(hop).start()
    maps_ref[:, pl.ds(pl.multiple_of(me * rows, SUBLANES), rows), :] = sens_ref[
        pl.ds(me * coils, coils)
    ]
    landed_ref[me] = packed_ref[me]

    row_pair = (row_top[...], row_low[...])
    col_pair = (col_top[...], col_low[...])
    for coil in range(coils):
        data_copy(coil).wait()
        for frame in range(frames):
            masked = data_ref[coil, :, frame, :] * mask_ref[:, frame : frame + 1]
            mid = dot3(split(masked), col_pair)
            both = dot3(row_pair, split(mid))
            base_ref[coil, frame, :, :half] = both[:length, :half] + both[length:, half:]
            base_ref[coil, frame, :, half:] = both[:length, half:] - both[length:, :half]
    for hop in range(1, devices):
        maps_copy(hop).wait()

    def copy_to(source, target, frame, slot, peer):
        return pltpu.make_async_remote_copy(
            src_ref=source,
            dst_ref=target,
            send_sem=send_sem.at[frame, slot],
            recv_sem=recv_sem.at[frame, slot],
            device_id={"coil": peer},
            device_id_type=MESH,
        )

    def core_copy(frame):
        return copy_to(term_ref.at[frame, :, :, 1 - core], got_a.at[frame], frame, 0, core_peer)

    def side_copy(frame):
        return copy_to(sum_a.at[frame, :, 1 - side], got_b.at[frame], frame, 1, side_peer)

    def rank_copy(frame, hop):
        return copy_to(
            sum_b.at[frame, (rank + hop) % ranks],
            got_c.at[frame, hop - 1],
            frame,
            1 + hop,
            rank_peers[hop - 1],
        )

    def weigh(frame):
        real, imag = (0.0, 0.0)
        for coil in range(coils):
            base_re, base_im = (base_ref[coil, frame, :, :half], base_ref[coil, frame, :, half:])
            maps_re, maps_im = (maps_ref[coil, :, :half], maps_ref[coil, :, half:])
            real = real + maps_re * base_re + maps_im * base_im
            imag = imag + maps_re * base_im - maps_im * base_re
        shape = term_ref.shape[1:4] + (width, length)
        term_ref[frame, :, :, :, :width] = jnp.transpose(real).reshape(shape)
        term_ref[frame, :, :, :, width:] = jnp.transpose(imag).reshape(shape)

    def project(frame):
        cut = landed_ref.shape[2] - 2 * frames * width
        coil_shape = (cut // 2 // width, width, length)
        maps_re = columns_ref[: cut // 2].reshape(coil_shape)
        maps_im = columns_ref[cut // 2 : cut].reshape(coil_shape)
        first = cut + frame * width
        now_re = columns_ref[first : first + width][None]
        first = first + frames * width
        now_im = columns_ref[first : first + width][None]
        seen_re = (maps_re * now_re - maps_im * now_im).reshape(cut // 2, length)
        seen_im = (maps_re * now_im + maps_im * now_re).reshape(cut // 2, length)
        seen = split(jnp.concatenate([seen_re, seen_im], 1))
        real, imag = (real_ref[frame], imag_ref[frame])
        upper = jnp.concatenate([real, -imag], 1)
        lower = jnp.concatenate([imag, real], 1)
        kept = dot3(seen, split(jnp.concatenate([upper, lower], 0)))
        kept_re = kept[:, :length].reshape(coil_shape)
        kept_im = kept[:, length:].reshape(coil_shape)
        grad_ref[0, frame] = jnp.sum(maps_re * kept_re + maps_im * kept_im, 0)
        grad_ref[1, frame] = jnp.sum(maps_re * kept_im - maps_im * kept_re, 0)

    for turn in range(frames + 3):
        if turn == 3:
            for hop in range(1, devices):
                pack_copy(hop).wait()
            columns_ref[...] = jnp.transpose(
                landed_ref[...].reshape(length, landed_ref.shape[2])
            )
        if turn < frames:
            weigh(turn)
            core_copy(turn).start()
        if 0 <= turn - 1 < frames:
            frame = turn - 1
            core_copy(frame).wait()
            sum_a[frame] = term_ref[frame, :, :, core] + got_a[frame]
            side_copy(frame).start()
        if 0 <= turn - 2 < frames:
            frame = turn - 2
            side_copy(frame).wait()
            sum_b[frame] = sum_a[frame, :, side] + got_b[frame]
            for hop in range(1, ranks):
                rank_copy(frame, hop).start()
        if turn - 3 >= 0:
            frame = turn - 3
            total = sum_b[frame, rank]
            for hop in range(1, ranks):
                rank_copy(frame, hop).wait()
                total = total + got_c[frame, hop - 1]
            out_ref[0, frame] = total[:width]
            out_ref[1, frame] = total[width:]
        if turn >= 3:
            project(turn - 3)


def gather(image, sens, kspace, mask, devices, tables, real, imag):
    rows, frames, packed = image.shape
    length, pairs, unused = kspace.shape
    coils = pairs // frames
    ranks = devices // 4
    width = packed // 2 // devices
    lanes = 2 * (sens.shape[1] + frames) * width
    row_cos, row_sin, col_cos, col_sin = tables
    row_pair = narrow(jnp.concatenate([row_cos, row_sin], 0))
    col_pair = narrow(column_matrix(col_cos, -col_sin))
    block = (2 * width, length)
    whole = pl.BlockSpec(memory_space=pltpu.VMEM)

    def held(*shape):
        return pltpu.VMEM(shape, jnp.float32)

    dma = pltpu.SemaphoreType.DMA
    return pl.pallas_call(
        lambda *refs: gather_kernel(devices, *refs),
        out_shape=(
            jax.ShapeDtypeStruct((2, frames, width, length), jnp.float32),
            jax.ShapeDtypeStruct((lanes, length), jnp.float32),
            jax.ShapeDtypeStruct((2, frames, width, length), jnp.float32),
        ),
        in_specs=[whole] * 2 + [pl.BlockSpec(memory_space=pl.ANY)] + [whole] * 7,
        out_specs=(whole, whole, whole),
        scratch_shapes=[
            held(coils, length, frames, packed),
            held(coils, frames, length, packed),
            held(coils, length, packed),
            held(devices, rows, lanes),
            held(devices, rows, lanes),
            held(frames, ranks, 2, 2, *block),
            held(frames, ranks, 2, *block),
            held(frames, ranks, 2, *block),
            held(frames, ranks, *block),
            held(frames, ranks, *block),
            held(frames, ranks - 1, *block),
            dma((frames, ranks + 1)),
            dma((frames, ranks + 1)),
            dma((devices - 1,)),
            dma((devices - 1,)),
            dma((devices - 1,)),
            dma((devices - 1,)),
            dma((coils,)),
        ],
        compiler_params=pltpu.CompilerParams(
            collective_id=0, has_side_effects=True, vmem_limit_bytes=60 * 1024 * 1024
        ),
        name="gather_reduce",
    )(
        jnp.transpose(sens, (1, 0, 2)),
        jnp.transpose(image, (1, 0, 2)),
        kspace,
        jnp.transpose(mask),
        *row_pair,
        *col_pair,
        real,
        imag,
    )


def return_kernel(devices, width, field_ref, out_ref, ready, landed, send_sem, recv_sem):
    rows, frames, unused = out_ref.shape
    group = LANES // width
    half = devices * width
    me = lax.axis_index("coil")
    peers = [(me + hop) % devices for hop in range(1, devices)]
    turned = jnp.transpose(field_ref[...])
    ready[...] = turned.reshape(devices, rows, turned.shape[1])
    greet(peers)
    copies = []
    for hop in range(1, devices):
        copies.append(
            pltpu.make_async_remote_copy(
                src_ref=ready.at[peers[hop - 1]],
                dst_ref=landed.at[me],
                send_sem=send_sem.at[hop - 1],
                recv_sem=recv_sem.at[hop - 1],
                device_id={"coil": peers[hop - 1]},
                device_id_type=MESH,
            )
        )
        copies[-1].start()
    landed[me] = ready[me]
    for copy in copies:
        copy.wait()
    for part in range(2):
        for first in range(0, frames, group):
            lane = (part * frames + first) * width
            for tile in range(devices // group):
                taken = [landed[tile * group + at, :, lane : lane + LANES] for at in range(group)]
                target = part * half + tile * LANES
                for at, value in enumerate(swap_blocks(taken, width)):
                    out_ref[:, first + at, target : target + LANES] = value


def return_rows(field, devices, rows):
    unused, frames, width, length = field.shape
    lanes = 2 * frames * width
    return pl.pallas_call(
        lambda *refs: return_kernel(devices, width, *refs),
        out_shape=jax.ShapeDtypeStruct((rows, frames, 2 * width * devices), jnp.float32),
        in_specs=[pl.BlockSpec(memory_space=pltpu.VMEM)],
        out_specs=pl.BlockSpec(memory_space=pltpu.VMEM),
        scratch_shapes=[
            pltpu.VMEM((devices, rows, lanes), jnp.float32),
            pltpu.VMEM((devices, rows, lanes), jnp.float32),
            pltpu.SemaphoreType.DMA((devices - 1,)),
            pltpu.SemaphoreType.DMA((devices - 1,)),
        ],
        compiler_params=pltpu.CompilerParams(collective_id=1, has_side_effects=True),
        name="return_rows",
    )(field.reshape(lanes, length))


def split(value):
    top = value.astype(jnp.bfloat16)
    return (top, (value - top.astype(jnp.float32)).astype(jnp.bfloat16))


def narrow(value):
    top = lax.reduce_precision(value, 8, 7)
    return (top.astype(jnp.bfloat16), (value - top).astype(jnp.bfloat16))


def dot3(left, right):
    def one(a, b):
        return jnp.dot(a, b, preferred_element_type=jnp.float32)

    return one(left[1], right[0]) + one(left[0], right[1]) + one(left[0], right[0])


def per_device(image, sens, kspace, mask):
    devices = lax.axis_size("coil")
    device = lax.axis_index("coil")
    rows_dev, frames, packed = image.shape
    coils = sens.shape[1]
    length, pairs, unused = kspace.shape
    half = packed // 2
    width = half // devices
    copies = max(1, frames // pairs)
    own_coils = max(1, pairs // frames)
    own_frames = min(frames, pairs)
    row_cos, row_sin = dft_tables(length)
    col_cos, col_sin = dft_tables(half)

    mask_float = mask.astype(jnp.float32)
    real, imag = projections(mask, row_cos, row_sin)
    opening = None
    fits = blocked(devices, width, rows_dev, (coils, frames)) and own_frames == frames
    fits = fits and devices % 8 == 0 and frames % SUBLANES == 0
    if fits:
        tables = (row_cos, row_sin, col_cos, col_sin)
        data_term, columns, opening = gather(
            image, sens, kspace, mask_float, devices, tables, real, imag
        )
    else:
        spread = sens if copies == 1 else jnp.repeat(sens, copies, axis=1)
        own_maps = lax.all_to_all(spread, "coil", split_axis=1, concat_axis=0, tiled=True)
        outgoing = jnp.concatenate([to_columns(sens, devices), to_columns(image, devices)], 2)
        incoming = lax.all_to_all(outgoing, "coil", split_axis=0, concat_axis=0, tiled=True)
        columns = jnp.transpose(incoming.reshape(length, -1))
        first_frame = device * pairs % frames
        local_mask = lax.dynamic_slice_in_dim(mask_float, first_frame, own_frames, 0)
        mask_pairs = jnp.tile(local_mask, (own_coils, 1))
        base_re, base_im = data_images(kspace, mask_pairs, row_cos, row_sin, col_cos, col_sin)
        base_re = base_re.reshape(length, own_coils, own_frames, half)
        base_im = base_im.reshape(length, own_coils, own_frames, half)
        own_re, own_im = (own_maps[:, :, None, :half], own_maps[:, :, None, half:])
        term_re = jnp.sum(own_re * base_re + own_im * base_im, 1)
        term_im = jnp.sum(own_re * base_im - own_im * base_re, 1)
        term = jnp.transpose(jnp.stack([term_re, term_im]), (3, 0, 2, 1))
        if own_frames < frames:
            wide = jnp.zeros((half, 2, frames, length), jnp.float32)
            term = lax.dynamic_update_slice_in_dim(wide, term, first_frame, 2)
        term = term.reshape(devices, width, 2, frames, length)
        data_term = lax.psum_scatter(term, "coil", scatter_dimension=0, tiled=True)
        data_term = jnp.transpose(data_term[0], (1, 2, 0, 3))

    cut = 2 * coils * width
    maps = columns[:cut].reshape(2, coils, width, length)
    field = columns[cut:].reshape(2, frames, width, length)
    field = iterate(field, data_term, maps, real, imag, opening)

    if fits:
        return return_rows(field, devices, rows_dev)
    leaving = jnp.transpose(field.reshape(2 * frames * width, length))
    leaving = leaving.reshape(devices, rows_dev, 2 * frames * width)
    arrived = lax.all_to_all(leaving, "coil", split_axis=0, concat_axis=0, tiled=True)
    arrived = arrived.reshape(devices, rows_dev, 2, frames, width)
    return jnp.transpose(arrived, (1, 3, 2, 0, 4)).reshape(rows_dev, frames, packed)


def solution(mesh):
    return jax.shard_map(
        per_device,
        mesh=mesh,
        in_specs=(
            P(("plane", "coil"), None, None),
            P(("plane", "coil"), None, None),
            P("plane", "coil", None),
            P(),
        ),
        out_specs=P(("plane", "coil"), None, None),
        check_vma=False,
    )
```
